32 devices in a mesh: rows: 16 (over z, x, core), feat: 2 (over y).
Axes of the slice: x: 2, y: 2, z: 4, core: 2. Of those that a mesh axis runs over, the one named last changes fastest.
Arguments:
- design: bfloat16 [16384, 16384], P('rows', 'feat'), may hold values from -6 to 6
- flags: int32 [16384], P('rows'), may hold values 0 or 1
- scales: float32 [16384], P('rows'), may hold values from 0.3 to 3
- damping: float32 [2, 8192], P('feat', 'rows'), may hold values from 0.2 to 2
- probes: float32 [32, 2, 8192], P(None, 'feat', 'rows'), may hold values from -6 to 6
Outputs:
- solution: float32 [32, 2, 8192], P(None, 'feat', 'rows')
- residual: float32 [32, 2, 8192], P(None, 'feat', 'rows')
The draws below stay inside these ranges and needn't reach their ends.
All inputs are finite; a program needn't handle non-finite values. No bound on the sum of `flags` on one device may be relied on, other than what follows from the above.
Results may differ from the reference program's by a relative error of at most 0.0073.
Values may be sent and summed in bfloat16 or wider, within the bound.
A program may use at most 64 MiB of HBM per device.

```python
import math
import jax
import jax.numpy as jnp
from jax import lax

F = 16384
K = 32
ITERS = 2
ROWS = 16384
FB = 8192
N_FEAT = 2


def set_ends(values, own_key, least, top_value):
    shape = values.shape
    index_at = [jax.random.randint(jax.random.fold_in(own_key, axis), (), 0, shape[axis]) for axis in range(len(shape))]
    values = values.at[tuple(index_at)].set(least)
    longest = shape.index(max(shape))
    index_at[longest] = (index_at[longest] + 1) % shape[longest]
    return values.at[tuple(index_at)].set(top_value)


def block_scale(stream_key, shape, shards, low, largest):
    loudness, own = 1.0, jax.random.fold_in(stream_key, 6)
    for position, parts in shards:
        heights = jnp.exp(jax.random.uniform(jax.random.fold_in(own, position), (parts,), jnp.float32, low / len(shards), largest / len(shards)))
        loudness = loudness * jnp.repeat(heights, shape[position] // parts).reshape([-1 if axis == position else 1 for axis in range(len(shape))])
    return loudness


def centred(own_key, extent, deviation, bound, cuts=(), held_as=jnp.bfloat16):
    values = jax.random.normal(own_key, extent, jnp.float32) * deviation
    if len(cuts) > 0:
        values = block_scale(own_key, extent, cuts, -0.22, 0.18) * values
    return jnp.clip(values, min=-bound, max=bound).astype(held_as)


def setup_inputs(seed: int = 0) -> dict:
    seeds = jax.random.split(jax.random.key(seed), 6)
    design = centred(seeds[0], (ROWS, F), 1.0, 6.0, ((0, 16), (1, 2)))
    flags = set_ends((jax.random.randint(seeds[1], (ROWS,), 0, 10) < 7).astype(jnp.int32), jax.random.fold_in(seeds[1], 1), 0, 1)
    scales = jnp.clip(jnp.exp(math.log(3.0) - 2.3025851 * jax.random.uniform(seeds[2], (ROWS,), jnp.float32) ** block_scale(seeds[2], (ROWS,), ((0, 16),), -0.2, 0.2)), 0.3, 3.0)
    damping = jnp.clip(jnp.exp(math.log(2.0) - 2.3025851 * jax.random.uniform(seeds[3], (N_FEAT, FB), jnp.float32) ** block_scale(seeds[3], (N_FEAT, FB), ((0, 2), (1, 16)), -0.2, 0.2)), 0.2, 2.0)
    probes = centred(seeds[4], (K, N_FEAT, FB), 1.0, 6.0, ((1, 2), (2, 16)), jnp.float32)
    return {"design": design, "flags": flags, "scales": scales, "damping": damping, "probes": probes}


def hessian(design, wrow, damp, direction):
    p_low = direction.astype(jnp.bfloat16)
    prod = lax.dot_general(p_low, design, (((1,), (1,)), ((), ())), preferred_element_type=jnp.float32)
    weighted = (wrow[None, :] * prod).astype(jnp.bfloat16)
    back = jnp.dot(weighted, design, preferred_element_type=jnp.float32)
    return back + damp[None, :] * direction


def reference(design, flags, scales, damping, probes):
    wrow = flags.astype(jnp.float32) / (scales * scales) / ROWS
    damp = damping.reshape(-1)
    rhs = probes.reshape(probes.shape[0], -1)
    solution = jnp.zeros_like(rhs)
    residual = rhs
    direction = rhs
    norm_now = jnp.sum(residual * residual, axis=1)
    for step in range(ITERS):
        image = hessian(design, wrow, damp, direction)
        alpha = norm_now / jnp.sum(direction * image, axis=1)
        solution = solution + alpha[:, None] * direction
        residual = residual - alpha[:, None] * image
        norm_next = jnp.sum(residual * residual, axis=1)
        direction = residual + (norm_next / norm_now)[:, None] * direction
        norm_now = norm_next
    return solution.reshape(probes.shape), residual.reshape(probes.shape)
```

```python
import functools

import jax
import jax.numpy as jnp
from jax import lax
from jax.experimental import pallas as pl
from jax.experimental.pallas import tpu as pltpu
from jax.sharding import PartitionSpec as P

ITERS = 2
MESH = pl.DeviceIdType.MESH
F32 = jnp.float32
BF16 = jnp.bfloat16


def weigh(partial_value, wrow):
    summed = lax.psum(partial_value, "feat")
    return (wrow[None, :] * summed).astype(jnp.bfloat16)


def norms_block(resid):
    return lax.psum(jnp.sum(resid * resid, axis=1), "feat")


def shards(design, flags, scales, damping, probes):
    rows_dev = design.shape[0]
    total_rows = rows_dev * lax.axis_size("rows")
    wrow = flags.astype(jnp.float32) / (scales * scales) / total_rows
    columns = probes.shape[0]
    damp_full, rhs_full = (
        lax.all_gather(damping, "rows", axis=1, tiled=True),
        lax.all_gather(probes, "rows", axis=2, tiled=True),
    )
    damp = damp_full.reshape(-1)
    rhs = rhs_full.reshape(columns, -1)
    solution = jnp.zeros_like(rhs)
    residual = rhs
    direction = rhs
    norm_now = norms_block(residual)
    for step in range(ITERS):
        p_low = direction.astype(jnp.bfloat16)
        partial_value = lax.dot_general(
            p_low, design, (((1,), (1,)), ((), ())), preferred_element_type=jnp.float32
        )
        weighted = weigh(partial_value, wrow)
        term = jnp.dot(weighted, design, preferred_element_type=jnp.float32)
        image = lax.psum(term, "rows") + damp[None, :] * direction
        curve = lax.psum(jnp.sum(direction * image, axis=1), "feat")
        alpha = norm_now / curve
        solution = solution + alpha[:, None] * direction
        residual = residual - alpha[:, None] * image
        norm_next = norms_block(residual)
        direction = residual + (norm_next / norm_now)[:, None] * direction
        norm_now = norm_next
    width = probes.shape[2]
    offset = lax.axis_index("rows") * width
    own_solution = lax.dynamic_slice_in_dim(solution, offset, width, 1)
    own_residual = lax.dynamic_slice_in_dim(residual, offset, width, 1)
    return (own_solution.reshape(probes.shape), own_residual.reshape(probes.shape))


def solve_kernel(
    depth, a_hbm, w_ref, d_ref, b_ref, x_ref, r_ref,
    a, g, st, y, yr, yold, ss, ssr, ds, dr, xs, xr, zs, zr, tt, cs, cx, cz, p_ref,
    a_sem, gs, gr, ss_s, ss_r, fs, fr, d_s, d_r, x_s, x_r, z_s, z_r, c_s, c_r,
):
    n = depth * 4
    cols, width = b_ref.shape
    me = lax.axis_index("rows")
    feat = lax.axis_index("feat")
    core = lax.rem(me, 2)
    xx = lax.rem(me // 2, 2)
    zz = me // 4

    def rows_of(slot):
        dz, dx, dc = slot // 4, (slot // 2) % 2, slot % 2
        z1 = lax.rem(zz + dz, depth)
        x1 = 1 - xx if dx else xx
        c1 = 1 - core if dc else core
        return (z1 * 2 + x1) * 2 + c1

    def dev(slot):
        return (rows_of(slot), feat)

    other_feat = (me, 1 - feat)

    far = list(range(1, depth))
    order = [0, 1, 2] + [4 * k for k in far] + [3]
    for e in (1, 2, 3):
        order += [4 * k + e for k in far]

    def load(slot):
        start = pl.multiple_of(rows_of(slot) * width, width)
        return pltpu.make_async_copy(
            a_hbm.at[:, pl.ds(start, width)], a.at[slot], a_sem.at[slot]
        )

    for slot in order:
        load(slot).start()

    peers = [dev(1), dev(2)] + [dev(4 * k) for k in far] + [other_feat]
    barrier = pltpu.get_barrier_semaphore()
    for peer in peers:
        pl.semaphore_signal(barrier, inc=1, device_id=peer, device_id_type=MESH)
    pl.semaphore_wait(barrier, len(peers))

    mask = lax.broadcasted_iota(jnp.int32, (cols, 128), 0) == lax.broadcasted_iota(
        jnp.int32, (cols, 128), 1
    )

    def to_row(v):
        return jnp.sum(jnp.where(mask, v, 0.0), axis=0, keepdims=True)

    def to_col(t):
        return jnp.sum(jnp.where(mask, t, 0.0), axis=1, keepdims=True)

    def remote(src, dst, send, recv, target):
        return pltpu.make_async_remote_copy(
            src_ref=src, dst_ref=dst, send_sem=send, recv_sem=recv,
            device_id=target, device_id_type=MESH,
        )

    x_ref[...] = jnp.zeros((cols, width), F32)
    p_ref[...] = jnp.zeros((cols, width), F32)
    r_ref[...] = b_ref[...]
    yold[...] = jnp.zeros_like(yold)

    def iteration(it, carry):
        rr_old, dpp_old = carry
        sent = []

        def share(src_slot, dst_slot, target):
            block = remote(
                g.at[it, src_slot], g.at[it, dst_slot],
                gs.at[it, dst_slot], gr.at[it, dst_slot], dev(target),
            )
            sums = remote(
                st.at[it, src_slot], st.at[it, dst_slot],
                ss_s.at[it, dst_slot], ss_r.at[it, dst_slot], dev(target),
            )
            block.start()
            sums.start()
            sent.extend([block, sums])

        def arrive(slot):
            remote(
                g.at[it, slot], g.at[it, slot], gs.at[it, slot], gr.at[it, slot], dev(1)
            ).wait_recv()
            remote(
                st.at[it, slot], st.at[it, slot],
                ss_s.at[it, slot], ss_r.at[it, slot], dev(1),
            ).wait_recv()

        r = r_ref[...]
        p = p_ref[...]
        damp = d_ref[...]
        g[it, 0] = r.astype(BF16)
        dr_ = damp * r
        st[it, 0] = jnp.zeros((8, 128), F32)
        st[it, 0, 0:1] = to_row(jnp.sum(r * r, axis=1, keepdims=True))
        st[it, 0, 1:2] = to_row(jnp.sum(dr_ * r, axis=1, keepdims=True))
        st[it, 0, 2:3] = to_row(jnp.sum(dr_ * p, axis=1, keepdims=True))

        for k in far:
            share(0, 4 * (depth - k), 4 * k)
        share(0, 2, 2)
        share(0, 1, 1)

        def product(slot, first=False):
            @pl.when(it == 0)
            def _():
                load(slot).wait()

            part = lax.dot_general(
                g[it, slot], a[slot], (((1,), (1,)), ((), ())),
                preferred_element_type=F32,
            )
            if first:
                y[...] = part
            else:
                y[...] += part

        product(0, True)
        arrive(1)
        product(1)
        arrive(2)
        share(2, 3, 1)
        for k in far:
            arrive(4 * k)
            share(4 * k, 4 * k + 2, 2)
            share(4 * k, 4 * k + 1, 1)
        product(2)
        for k in far:
            product(4 * k)
        arrive(3)
        product(3)
        for k in far:
            arrive(4 * k + 2)
            share(4 * k + 2, 4 * k + 3, 1)
        for k in far:
            arrive(4 * k + 1)
            product(4 * k + 1)
        for k in far:
            product(4 * k + 2)
        for k in far:
            arrive(4 * k + 3)
            product(4 * k + 3)

        yc = remote(y, yr.at[it], fs.at[it, 0], fr.at[it, 0], other_feat)
        yc.start()
        total = st[it, 0]
        for slot in range(1, n):
            total = total + st[it, slot]
        ss[it] = total
        sc = remote(ss.at[it], ssr.at[it], fs.at[it, 1], fr.at[it, 1], other_feat)
        sc.start()
        sc.wait_recv()
        sums = total + ssr[it]
        rr = to_col(sums[0:1])
        drr = to_col(sums[1:2])
        drp = to_col(sums[2:3])
        beta = jnp.where(it == 0, 0.0, rr / rr_old)
        dpp = drr + 2.0 * beta * drp + beta * beta * dpp_old
        p = r + beta * p
        p_ref[...] = p
        yc.wait_recv()
        yy = y[...] + yr[it] + beta * yold[...]
        yold[...] = yy
        wy = w_ref[...] * yy
        u = wy.astype(BF16)
        curve_own = to_row(jnp.sum(wy * yy, axis=1, keepdims=True))
        cs[it, 0] = jnp.broadcast_to(curve_own, (8, 128))

        def small(src, dst, k, target):
            copy = remote(src, dst, c_s.at[it, k], c_r.at[it, k], dev(target))
            copy.start()
            sent.append(copy)
            return copy

        c_die = small(cs.at[it, 0], cs.at[it, 1], 0, 1)

        def term(slot):
            return jnp.dot(u, a[slot], preferred_element_type=F32)

        def to_die(k, dx):
            i = 2 * k + dx
            ds[it, i] = term(4 * k + 2 * dx + 1)
            copy = remote(ds.at[it, i], dr.at[it, i], d_s.at[it, i], d_r.at[it, i], dev(1))
            copy.start()
            sent.append(copy)

        def from_die(k, dx):
            i = 2 * k + dx
            remote(
                ds.at[it, i], dr.at[it, i], d_s.at[it, i], d_r.at[it, i], dev(1)
            ).wait_recv()
            return dr[it, i]

        zorder = far + [0]
        for k in zorder:
            to_die(k, 1)
        c_die.wait_recv()
        c_pair = cs[it, 0] + cs[it, 1]
        cx[it, 0] = c_pair
        c_x = small(cx.at[it, 0], cx.at[it, 1], 1, 2)
        for k in zorder:
            part = term(4 * k + 2)
            xs[it, k] = (part + from_die(k, 1)).astype(BF16)
            copy = remote(xs.at[it, k], xr.at[it, k], x_s.at[it, k], x_r.at[it, k], dev(2))
            copy.start()
            sent.append(copy)
        for k in zorder:
            to_die(k, 0)
        c_x.wait_recv()
        c_chip = cx[it, 0] + cx[it, 1]
        cz[it, 0] = c_chip
        c_z = [small(cz.at[it, 0], cz.at[it, depth - k], 1 + k, 4 * k) for k in far]
        for k in zorder:
            tt[k] = term(4 * k)

        def chip_sum(k):
            part = tt[k] + from_die(k, 0)
            remote(
                xs.at[it, k], xr.at[it, k], x_s.at[it, k], x_r.at[it, k], dev(2)
            ).wait_recv()
            return part + xr[it, k].astype(F32)

        for k in far:
            zs[it, k] = chip_sum(k).astype(BF16)
            copy = remote(
                zs.at[it, k], zr.at[it, depth - k],
                z_s.at[it, k], z_r.at[it, depth - k], dev(4 * k),
            )
            copy.start()
            sent.append(copy)
        image = chip_sum(0) + damp * p
        curve_row = cz[it, 0]
        for k in far:
            remote(
                cz.at[it, 0], cz.at[it, k], c_s.at[it, 1 + k], c_r.at[it, 1 + depth - k],
                dev(4 * k),
            ).wait_recv()
            curve_row = curve_row + cz[it, k]
        alpha = rr / (to_col(curve_row[0:1]) + dpp)
        x_ref[...] += alpha * p
        for k in far:
            remote(
                zs.at[it, k], zr.at[it, k], z_s.at[it, k], z_r.at[it, k], dev(4 * k)
            ).wait_recv()
            image = image + zr[it, k].astype(F32)
        r_ref[...] = r - alpha * image

        yc.wait_send()
        sc.wait_send()
        for copy in sent:
            copy.wait_send()
        return rr, dpp

    ones = jnp.ones((cols, 1), F32)
    lax.fori_loop(0, ITERS, iteration, (ones, jnp.zeros((cols, 1), F32)))


def fused(depth, design, flags, scales, damping, probes):
    rows_dev = design.shape[0]
    n = depth * 4
    total_rows = rows_dev * n
    wrow = flags.astype(F32) / (scales * scales) / total_rows
    cols, _, width = probes.shape
    vm = pl.BlockSpec(memory_space=pltpu.VMEM)
    v = pltpu.VMEM
    dma = pltpu.SemaphoreType.DMA
    out = jax.ShapeDtypeStruct((cols, width), F32)
    i2 = ITERS
    x, r = pl.pallas_call(
        functools.partial(solve_kernel, depth),
        out_shape=(out, out),
        in_specs=[pl.BlockSpec(memory_space=pl.ANY), vm, vm, vm],
        out_specs=(vm, vm),
        scratch_shapes=[
            v((n, rows_dev, width), BF16),
            v((i2, n, cols, width), BF16),
            v((i2, n, 8, 128), F32),
            v((cols, rows_dev), F32),
            v((i2, cols, rows_dev), F32),
            v((cols, rows_dev), F32),
            v((i2, 8, 128), F32),
            v((i2, 8, 128), F32),
            v((i2, 2 * depth, cols, width), F32),
            v((i2, 2 * depth, cols, width), F32),
            v((i2, depth, cols, width), BF16),
            v((i2, depth, cols, width), BF16),
            v((i2, depth, cols, width), BF16),
            v((i2, depth, cols, width), BF16),
            v((depth, cols, width), F32),
            v((i2, 2, 8, 128), F32),
            v((i2, 2, 8, 128), F32),
            v((i2, depth, 8, 128), F32),
            v((cols, width), F32),
            dma((n,)),
            dma((i2, n)),
            dma((i2, n)),
            dma((i2, n)),
            dma((i2, n)),
            dma((i2, 2)),
            dma((i2, 2)),
            dma((i2, 2 * depth)),
            dma((i2, 2 * depth)),
            dma((i2, depth)),
            dma((i2, depth)),
            dma((i2, depth)),
            dma((i2, depth)),
            dma((i2, depth + 1)),
            dma((i2, depth + 1)),
        ],
        compiler_params=pltpu.CompilerParams(
            collective_id=0, has_side_effects=True, vmem_limit_bytes=48 * 1024 * 1024
        ),
    )(design, wrow.reshape(1, rows_dev), damping, probes.reshape(cols, width))
    return x.reshape(probes.shape), r.reshape(probes.shape)


def solution(mesh):
    placed = (P("rows", "feat"), P("rows"), P("rows"), P("feat", "rows"), P(None, "feat", "rows"))
    rows, feats = mesh.shape["rows"], mesh.shape["feat"]

    def body(design, flags, scales, damping, probes):
        fits = (
            feats == 2 and rows % 4 == 0 and 8 <= rows <= 16
            and probes.shape[2] % 256 == 0 and design.shape[0] % 256 == 0
            and design.size <= 1 << 23 and probes.shape[0] % 16 == 0
            and probes.shape[0] <= 32
        )
        if fits:
            return fused(rows // 4, design, flags, scales, damping, probes)
        return shards(design, flags, scales, damping, probes)

    return jax.shard_map(
        body,
        mesh=mesh,
        in_specs=placed,
        out_specs=(P(None, "feat", "rows"), P(None, "feat", "rows")),
        check_vma=False,
    )
```

```python
import functools

import jax
import jax.numpy as jnp
from jax import lax
from jax.experimental import pallas as pl
from jax.experimental.pallas import tpu as pltpu
from jax.sharding import PartitionSpec as P

ITERS = 2
MESH = pl.DeviceIdType.MESH
F32 = jnp.float32
BF16 = jnp.bfloat16


def weigh(partial_value, wrow):
    summed = lax.psum(partial_value, "feat")
    return (wrow[None, :] * summed).astype(jnp.bfloat16)


def norms_block(resid):
    return lax.psum(jnp.sum(resid * resid, axis=1), "feat")


def shards(design, flags, scales, damping, probes):
    rows_dev = design.shape[0]
    total_rows = rows_dev * lax.axis_size("rows")
    wrow = flags.astype(jnp.float32) / (scales * scales) / total_rows
    columns = probes.shape[0]
    damp_full, rhs_full = (
        lax.all_gather(damping, "rows", axis=1, tiled=True),
        lax.all_gather(probes, "rows", axis=2, tiled=True),
    )
    damp = damp_full.reshape(-1)
    rhs = rhs_full.reshape(columns, -1)
    solution = jnp.zeros_like(rhs)
    residual = rhs
    direction = rhs
    norm_now = norms_block(residual)
    for step in range(ITERS):
        p_low = direction.astype(jnp.bfloat16)
        partial_value = lax.dot_general(
            p_low, design, (((1,), (1,)), ((), ())), preferred_element_type=jnp.float32
        )
        weighted = weigh(partial_value, wrow)
        term = jnp.dot(weighted, design, preferred_element_type=jnp.float32)
        image = lax.psum(term, "rows") + damp[None, :] * direction
        curve = lax.psum(jnp.sum(direction * image, axis=1), "feat")
        alpha = norm_now / curve
        solution = solution + alpha[:, None] * direction
        residual = residual - alpha[:, None] * image
        norm_next = norms_block(residual)
        direction = residual + (norm_next / norm_now)[:, None] * direction
        norm_now = norm_next
    width = probes.shape[2]
    offset = lax.axis_index("rows") * width
    own_solution = lax.dynamic_slice_in_dim(solution, offset, width, 1)
    own_residual = lax.dynamic_slice_in_dim(residual, offset, width, 1)
    return (own_solution.reshape(probes.shape), own_residual.reshape(probes.shape))


def solve_kernel(
    depth, total_rows, a_hbm, flags_in, scales_in, d_in, b_in, x_ref, r_ref,
    flags_ref, scales_ref, d_ref, b_ref, w_ref,
    a, g, st, y, yr, yold, ss, ssr, ds, dr, xs, xr, zs, zr, tt, cs, p_ref,
    in_sem, a_sem, gs, gr, ss_s, ss_r, fs, fr, d_s, d_r, x_s, x_r, z_s, z_r, c_s, c_r,
):
    n = depth * 4
    cols, width = x_ref.shape
    me = lax.axis_index("rows")
    feat = lax.axis_index("feat")
    core = lax.rem(me, 2)
    xx = lax.rem(me // 2, 2)
    zz = me // 4

    def rows_of(dz, dx, dc):
        z1 = lax.rem(zz + dz, depth)
        x1 = 1 - xx if dx else xx
        c1 = 1 - core if dc else core
        return (z1 * 2 + x1) * 2 + c1

    def dev(dz, dx, dc):
        return (rows_of(dz, dx, dc), feat)

    die, side = dev(0, 0, 1), dev(0, 1, 0)

    other_feat = (me, 1 - feat)

    upper = (zz * 2) // depth
    far = list(range(1, depth))
    away = [k * upper + (depth - k) * (1 - upper) for k in far]
    near = [depth - k for k in away]

    def load(dz, e):
        start = pl.multiple_of(rows_of(dz, e // 2, e % 2) * width, width)
        slot = dz * 4 + e
        return pltpu.make_async_copy(
            a_hbm.at[:, pl.ds(start, width)], a.at[slot], a_sem.at[slot]
        )

    small_loads = [
        pltpu.make_async_copy(src, dst, in_sem.at[i])
        for i, (src, dst) in enumerate(
            [(b_in, b_ref), (d_in, d_ref), (flags_in, flags_ref), (scales_in, scales_ref)]
        )
    ]
    for copy in small_loads:
        copy.start()
    for e in range(3):
        load(0, e).start()
    for k in near:
        load(k, 0).start()
    load(0, 3).start()
    for e in range(1, 4):
        for k in near:
            load(k, e).start()

    peers = [die, side] + [dev(k, 0, 0) for k in far] + [other_feat]
    barrier = pltpu.get_barrier_semaphore()
    for peer in peers:
        pl.semaphore_signal(barrier, inc=1, device_id=peer, device_id_type=MESH)
    pl.semaphore_wait(barrier, len(peers))

    mask = lax.broadcasted_iota(jnp.int32, (cols, 128), 0) == lax.broadcasted_iota(
        jnp.int32, (cols, 128), 1
    )

    def to_row(v):
        return jnp.sum(jnp.where(mask, v, 0.0), axis=0, keepdims=True)

    def to_col(t):
        return jnp.sum(jnp.where(mask, t, 0.0), axis=1, keepdims=True)

    def remote(src, dst, send, recv, target):
        return pltpu.make_async_remote_copy(
            src_ref=src, dst_ref=dst, send_sem=send, recv_sem=recv,
            device_id=target, device_id_type=MESH,
        )

    x_ref[...] = jnp.zeros((cols, width), F32)
    p_ref[...] = jnp.zeros((cols, width), F32)
    for copy in small_loads:
        copy.wait()
    r_ref[...] = b_ref[:, 0, :]
    scale = scales_ref[...]
    w_ref[...] = flags_ref[...].astype(F32) / (scale * scale) / total_rows
    yold[...] = jnp.zeros_like(yold)

    def iteration(it, carry):
        rr_old, dpp_old = carry
        sent = []

        def share(src_slot, dst_slot, target):
            block = remote(
                g.at[it, src_slot], g.at[it, dst_slot],
                gs.at[it, dst_slot], gr.at[it, dst_slot], target,
            )
            block.start()
            sent.append(block)

        def arrive(slot):
            remote(
                g.at[it, slot], g.at[it, slot], gs.at[it, slot], gr.at[it, slot], die
            ).wait_recv()

        def tell(buf, send, recv, src, dst, k, target):
            copy = remote(
                buf.at[it, src], buf.at[it, dst], send.at[it, k], recv.at[it, k], target
            )
            copy.start()
            sent.append(copy)

        def hear(buf, send, recv, dst, k):
            remote(
                buf.at[it, dst], buf.at[it, dst], send.at[it, k], recv.at[it, k], die
            ).wait_recv()

        r = r_ref[...]
        p = p_ref[...]
        damp = d_ref[...]
        g[it, 0] = r.astype(BF16)
        for k in away:
            share(0, 4 * (depth - k), dev(k, 0, 0))
        share(0, 2, side)
        share(0, 1, die)

        def reduce_start(buf, send, recv):
            tell(buf, send, recv, 0, 1, 0, die)

        def reduce_x(buf, send, recv):
            hear(buf, send, recv, 1, 0)
            buf[it, 2] = buf[it, 0] + buf[it, 1]
            tell(buf, send, recv, 2, 3, 1, side)

        def reduce_z(buf, send, recv):
            hear(buf, send, recv, 3, 1)
            buf[it, 4] = buf[it, 2] + buf[it, 3]
            for k in far:
                tell(buf, send, recv, 4, 4 + depth - k, 1 + depth - k, dev(k, 0, 0))

        def reduce_end(buf, send, recv):
            total = buf[it, 4]
            for k in far:
                hear(buf, send, recv, 4 + k, 1 + k)
                total = total + buf[it, 4 + k]
            return total

        dr_ = damp * r
        st[it, 0] = jnp.zeros((8, 128), F32)
        st[it, 0, 0:1] = to_row(jnp.sum(r * r, axis=1, keepdims=True))
        st[it, 0, 1:2] = to_row(jnp.sum(dr_ * r, axis=1, keepdims=True))
        st[it, 0, 2:3] = to_row(jnp.sum(dr_ * p, axis=1, keepdims=True))
        reduce_start(st, ss_s, ss_r)

        def product(dz, e, first=False):
            slot = dz * 4 + e

            @pl.when(it == 0)
            def _():
                load(dz, e).wait()

            part = lax.dot_general(
                g[it, slot], a[slot], (((1,), (1,)), ((), ())),
                preferred_element_type=F32,
            )
            if first:
                y[...] = part
            else:
                y[...] += part

        product(0, 0, True)
        reduce_x(st, ss_s, ss_r)
        arrive(1)
        product(0, 1)
        arrive(2)
        share(2, 3, die)
        for k in near:
            arrive(4 * k)
            share(4 * k, 4 * k + 2, side)
            share(4 * k, 4 * k + 1, die)
        reduce_z(st, ss_s, ss_r)
        product(0, 2)
        for k in near:
            product(k, 0)
        arrive(3)
        product(0, 3)
        for k in near:
            arrive(4 * k + 2)
            share(4 * k + 2, 4 * k + 3, die)
        for k in near:
            arrive(4 * k + 1)
            product(k, 1)
        for k in near:
            product(k, 2)
        for k in near:
            arrive(4 * k + 3)
            product(k, 3)

        yc = remote(y, yr.at[it], fs.at[it, 0], fr.at[it, 0], other_feat)
        yc.start()
        total = reduce_end(st, ss_s, ss_r)
        ss[it] = total
        sc = remote(ss.at[it], ssr.at[it], fs.at[it, 1], fr.at[it, 1], other_feat)
        sc.start()
        sc.wait_recv()
        sums = total + ssr[it]
        rr = to_col(sums[0:1])
        drr = to_col(sums[1:2])
        drp = to_col(sums[2:3])
        beta = jnp.where(it == 0, 0.0, rr / rr_old)
        dpp = drr + 2.0 * beta * drp + beta * beta * dpp_old
        p = r + beta * p
        p_ref[...] = p
        yc.wait_recv()
        yy = y[...] + yr[it] + beta * yold[...]
        yold[...] = yy
        wy = w_ref[...] * yy
        u = wy.astype(BF16)
        curve_own = to_row(jnp.sum(wy * yy, axis=1, keepdims=True))
        cs[it, 0] = jnp.broadcast_to(curve_own, (8, 128))

        reduce_start(cs, c_s, c_r)

        def term(slot):
            return jnp.dot(u, a[slot], preferred_element_type=F32)

        def to_die(k, dx):
            i = 2 * k + dx
            ds[it, i] = term(4 * k + 2 * dx + 1)
            copy = remote(ds.at[it, i], dr.at[it, i], d_s.at[it, i], d_r.at[it, i], die)
            copy.start()
            sent.append(copy)

        def from_die(k, dx):
            i = 2 * k + dx
            remote(
                ds.at[it, i], dr.at[it, i], d_s.at[it, i], d_r.at[it, i], die
            ).wait_recv()
            return dr[it, i]

        zorder = away + [0]
        for k in zorder:
            to_die(k, 1)
        reduce_x(cs, c_s, c_r)
        for k in zorder:
            part = term(4 * k + 2)
            xs[it, k] = (part + from_die(k, 1)).astype(BF16)
            copy = remote(xs.at[it, k], xr.at[it, k], x_s.at[it, k], x_r.at[it, k], side)
            copy.start()
            sent.append(copy)
        for k in zorder:
            to_die(k, 0)
        reduce_z(cs, c_s, c_r)
        for k in zorder:
            tt[k] = term(4 * k)

        def chip_sum(k):
            part = tt[k] + from_die(k, 0)
            remote(
                xs.at[it, k], xr.at[it, k], x_s.at[it, k], x_r.at[it, k], side
            ).wait_recv()
            return part + xr[it, k].astype(F32)

        for k in away:
            zs[it, k] = chip_sum(k).astype(BF16)
            copy = remote(
                zs.at[it, k], zr.at[it, depth - k],
                z_s.at[it, k], z_r.at[it, depth - k], dev(k, 0, 0),
            )
            copy.start()
            sent.append(copy)
        image = chip_sum(0) + damp * p
        curve_row = reduce_end(cs, c_s, c_r)
        alpha = rr / (to_col(curve_row[0:1]) + dpp)
        x_ref[...] += alpha * p
        for k in far:
            remote(
                zs.at[it, k], zr.at[it, k], z_s.at[it, k], z_r.at[it, k], die
            ).wait_recv()
            image = image + zr[it, k].astype(F32)
        r_ref[...] = r - alpha * image

        yc.wait_send()
        sc.wait_send()
        for copy in sent:
            copy.wait_send()
        return rr, dpp

    ones = jnp.ones((cols, 1), F32)
    lax.fori_loop(0, ITERS, iteration, (ones, jnp.zeros((cols, 1), F32)))


def fused(depth, design, flags, scales, damping, probes):
    rows_dev = design.shape[0]
    n = depth * 4
    total_rows = rows_dev * n
    cols, _, width = probes.shape
    vm = pl.BlockSpec(memory_space=pltpu.VMEM)
    v = pltpu.VMEM
    dma = pltpu.SemaphoreType.DMA
    out = jax.ShapeDtypeStruct((cols, width), F32)
    i2 = ITERS
    x, r = pl.pallas_call(
        functools.partial(solve_kernel, depth, total_rows),
        out_shape=(out, out),
        in_specs=[pl.BlockSpec(memory_space=pl.ANY)] * 5,
        out_specs=(vm, vm),
        scratch_shapes=[
            v((1, rows_dev), jnp.int32),
            v((1, rows_dev), F32),
            v((1, width), F32),
            v((cols, 1, width), F32),
            v((1, rows_dev), F32),
            v((n, rows_dev, width), BF16),
            v((i2, n, cols, width), BF16),
            v((i2, depth + 4, 8, 128), F32),
            v((cols, rows_dev), F32),
            v((i2, cols, rows_dev), F32),
            v((cols, rows_dev), F32),
            v((i2, 8, 128), F32),
            v((i2, 8, 128), F32),
            v((i2, 2 * depth, cols, width), F32),
            v((i2, 2 * depth, cols, width), F32),
            v((i2, depth, cols, width), BF16),
            v((i2, depth, cols, width), BF16),
            v((i2, depth, cols, width), BF16),
            v((i2, depth, cols, width), BF16),
            v((depth, cols, width), F32),
            v((i2, depth + 4, 8, 128), F32),
            v((cols, width), F32),
            dma((4,)),
            dma((n,)),
            dma((i2, n)),
            dma((i2, n)),
            dma((i2, depth + 1)),
            dma((i2, depth + 1)),
            dma((i2, 2)),
            dma((i2, 2)),
            dma((i2, 2 * depth)),
            dma((i2, 2 * depth)),
            dma((i2, depth)),
            dma((i2, depth)),
            dma((i2, depth)),
            dma((i2, depth)),
            dma((i2, depth + 1)),
            dma((i2, depth + 1)),
        ],
        compiler_params=pltpu.CompilerParams(
            collective_id=0, has_side_effects=True, vmem_limit_bytes=48 * 1024 * 1024
        ),
    )(design, flags.reshape(1, rows_dev), scales.reshape(1, rows_dev), damping, probes)
    return x.reshape(probes.shape), r.reshape(probes.shape)


def solution(mesh):
    placed = (P("rows", "feat"), P("rows"), P("rows"), P("feat", "rows"), P(None, "feat", "rows"))
    rows, feats = mesh.shape["rows"], mesh.shape["feat"]

    def body(design, flags, scales, damping, probes):
        fits = (
            feats == 2 and rows % 4 == 0 and 8 <= rows <= 16
            and probes.shape[2] % 256 == 0 and design.shape[0] % 256 == 0
            and design.size <= 1 << 23 and probes.shape[0] % 16 == 0
            and probes.shape[0] <= 32
        )
        if fits:
            return fused(rows // 4, design, flags, scales, damping, probes)
        return shards(design, flags, scales, damping, probes)

    return jax.shard_map(
        body,
        mesh=mesh,
        in_specs=placed,
        out_specs=(P(None, "feat", "rows"), P(None, "feat", "rows")),
        check_vma=False,
    )
```

```python
import functools

import jax
import jax.numpy as jnp
from jax import lax
from jax.experimental import pallas as pl
from jax.experimental.pallas import tpu as pltpu
from jax.sharding import PartitionSpec as P

ITERS = 2
MESH = pl.DeviceIdType.MESH
F32 = jnp.float32
BF16 = jnp.bfloat16


def weigh(partial_value, wrow):
    summed = lax.psum(partial_value, "feat")
    return (wrow[None, :] * summed).astype(jnp.bfloat16)


def norms_block(resid):
    return lax.psum(jnp.sum(resid * resid, axis=1), "feat")


def shards(design, flags, scales, damping, probes):
    rows_dev = design.shape[0]
    total_rows = rows_dev * lax.axis_size("rows")
    wrow = flags.astype(jnp.float32) / (scales * scales) / total_rows
    columns = probes.shape[0]
    damp_full, rhs_full = (
        lax.all_gather(damping, "rows", axis=1, tiled=True),
        lax.all_gather(probes, "rows", axis=2, tiled=True),
    )
    damp = damp_full.reshape(-1)
    rhs = rhs_full.reshape(columns, -1)
    solution = jnp.zeros_like(rhs)
    residual = rhs
    direction = rhs
    norm_now = norms_block(residual)
    for step in range(ITERS):
        p_low = direction.astype(jnp.bfloat16)
        partial_value = lax.dot_general(
            p_low, design, (((1,), (1,)), ((), ())), preferred_element_type=jnp.float32
        )
        weighted = weigh(partial_value, wrow)
        term = jnp.dot(weighted, design, preferred_element_type=jnp.float32)
        image = lax.psum(term, "rows") + damp[None, :] * direction
        curve = lax.psum(jnp.sum(direction * image, axis=1), "feat")
        alpha = norm_now / curve
        solution = solution + alpha[:, None] * direction
        residual = residual - alpha[:, None] * image
        norm_next = norms_block(residual)
        direction = residual + (norm_next / norm_now)[:, None] * direction
        norm_now = norm_next
    width = probes.shape[2]
    offset = lax.axis_index("rows") * width
    own_solution = lax.dynamic_slice_in_dim(solution, offset, width, 1)
    own_residual = lax.dynamic_slice_in_dim(residual, offset, width, 1)
    return (own_solution.reshape(probes.shape), own_residual.reshape(probes.shape))


def solve_kernel(
    depth, total_rows, a_hbm, flags_in, scales_in, d_in, b_in, x_ref, r_ref,
    flags_ref, scales_ref, d_ref, b_ref, w_ref,
    a, g, st, y, ylow, yr, yold, ss, ssr, ds, dr, xs, xr, zs, zr, tt, cs, p_ref,
    in_sem, a_sem, gs, gr, ss_s, ss_r, fs, fr, d_s, d_r, x_s, x_r, z_s, z_r, c_s, c_r,
):
    n = depth * 4
    cols, width = x_ref.shape
    me = lax.axis_index("rows")
    feat = lax.axis_index("feat")
    core = lax.rem(me, 2)
    xx = lax.rem(me // 2, 2)
    zz = me // 4

    def rows_of(dz, dx, dc):
        z1 = lax.rem(zz + dz, depth)
        x1 = 1 - xx if dx else xx
        c1 = 1 - core if dc else core
        return (z1 * 2 + x1) * 2 + c1

    def dev(dz, dx, dc):
        return (rows_of(dz, dx, dc), feat)

    die, side = dev(0, 0, 1), dev(0, 1, 0)

    other_feat = (me, 1 - feat)

    far = list(range(1, depth))
    away = far
    near = [depth - k for k in away]

    def load(dz, e):
        start = pl.multiple_of(rows_of(dz, e // 2, e % 2) * width, width)
        slot = dz * 4 + e
        return pltpu.make_async_copy(
            a_hbm.at[:, pl.ds(start, width)], a.at[slot], a_sem.at[slot]
        )

    small_loads = [
        pltpu.make_async_copy(src, dst, in_sem.at[i])
        for i, (src, dst) in enumerate(
            [(b_in, b_ref), (d_in, d_ref), (flags_in, flags_ref), (scales_in, scales_ref)]
        )
    ]
    for copy in small_loads:
        copy.start()
    for e in range(3):
        load(0, e).start()
    for k in near:
        load(k, 0).start()
    load(0, 3).start()
    for e in range(1, 4):
        for k in near:
            load(k, e).start()

    peers = [die, side] + [dev(k, 0, 0) for k in far] + [other_feat]
    barrier = pltpu.get_barrier_semaphore()
    for peer in peers:
        pl.semaphore_signal(barrier, inc=1, device_id=peer, device_id_type=MESH)
    pl.semaphore_wait(barrier, len(peers))

    mask = lax.broadcasted_iota(jnp.int32, (cols, 128), 0) == lax.broadcasted_iota(
        jnp.int32, (cols, 128), 1
    )

    def to_row(v):
        return jnp.sum(jnp.where(mask, v, 0.0), axis=0, keepdims=True)

    def to_col(t):
        return jnp.sum(jnp.where(mask, t, 0.0), axis=1, keepdims=True)

    def remote(src, dst, send, recv, target):
        return pltpu.make_async_remote_copy(
            src_ref=src, dst_ref=dst, send_sem=send, recv_sem=recv,
            device_id=target, device_id_type=MESH,
        )

    x_ref[...] = jnp.zeros((cols, width), F32)
    p_ref[...] = jnp.zeros((cols, width), F32)
    for copy in small_loads:
        copy.wait()
    r_ref[...] = b_ref[:, 0, :]
    scale = scales_ref[...]
    w_ref[...] = flags_ref[...].astype(F32) / (scale * scale) / total_rows
    yold[...] = jnp.zeros_like(yold)

    def iteration(it, carry):
        rr_old, dpp_old = carry
        sent = []

        def share(src_slot, dst_slot, target):
            block = remote(
                g.at[it, src_slot], g.at[it, dst_slot],
                gs.at[it, dst_slot], gr.at[it, dst_slot], target,
            )
            block.start()
            sent.append(block)

        def arrive(slot):
            remote(
                g.at[it, slot], g.at[it, slot], gs.at[it, slot], gr.at[it, slot], die
            ).wait_recv()

        def tell(buf, send, recv, src, dst, k, target):
            copy = remote(
                buf.at[it, src], buf.at[it, dst], send.at[it, k], recv.at[it, k], target
            )
            copy.start()
            sent.append(copy)

        def hear(buf, send, recv, dst, k):
            remote(
                buf.at[it, dst], buf.at[it, dst], send.at[it, k], recv.at[it, k], die
            ).wait_recv()

        r = r_ref[...]
        p = p_ref[...]
        damp = d_ref[...]
        g[it, 0] = r.astype(BF16)
        for k in away:
            share(0, 4 * (depth - k), dev(k, 0, 0))
        share(0, 2, side)
        share(0, 1, die)

        def reduce_start(buf, send, recv):
            tell(buf, send, recv, 0, 1, 0, die)

        def reduce_x(buf, send, recv):
            hear(buf, send, recv, 1, 0)
            buf[it, 2] = buf[it, 0] + buf[it, 1]
            tell(buf, send, recv, 2, 3, 1, side)

        def reduce_z(buf, send, recv):
            hear(buf, send, recv, 3, 1)
            buf[it, 4] = buf[it, 2] + buf[it, 3]
            for k in far:
                tell(buf, send, recv, 4, 4 + depth - k, 1 + depth - k, dev(k, 0, 0))

        def reduce_end(buf, send, recv):
            total = buf[it, 4]
            for k in far:
                hear(buf, send, recv, 4 + k, 1 + k)
                total = total + buf[it, 4 + k]
            return total

        dr_ = damp * r
        st[it, 0] = jnp.zeros((8, 128), F32)
        st[it, 0, 0:1] = to_row(jnp.sum(r * r, axis=1, keepdims=True))
        st[it, 0, 1:2] = to_row(jnp.sum(dr_ * r, axis=1, keepdims=True))
        st[it, 0, 2:3] = to_row(jnp.sum(dr_ * p, axis=1, keepdims=True))
        reduce_start(st, ss_s, ss_r)

        def product(dz, e, first=False):
            slot = dz * 4 + e

            @pl.when(it == 0)
            def _():
                load(dz, e).wait()

            part = lax.dot_general(
                g[it, slot], a[slot], (((1,), (1,)), ((), ())),
                preferred_element_type=F32,
            )
            if first:
                y[...] = part
            else:
                y[...] += part

        product(0, 0, True)
        reduce_x(st, ss_s, ss_r)
        arrive(1)
        product(0, 1)
        arrive(2)
        share(2, 3, die)
        for k in near:
            arrive(4 * k)
            share(4 * k, 4 * k + 2, side)
            share(4 * k, 4 * k + 1, die)
        reduce_z(st, ss_s, ss_r)
        product(0, 2)
        for k in near:
            product(k, 0)
        arrive(3)
        product(0, 3)
        for k in near:
            arrive(4 * k + 2)
            share(4 * k + 2, 4 * k + 3, die)
        for k in near:
            arrive(4 * k + 1)
            product(k, 1)
        for k in near:
            product(k, 2)
        for k in near:
            arrive(4 * k + 3)
            product(k, 3)

        ylow[...] = y[...].astype(BF16)
        yc = remote(ylow, yr.at[it], fs.at[it, 0], fr.at[it, 0], other_feat)
        yc.start()
        total = reduce_end(st, ss_s, ss_r)
        ss[it] = total
        sc = remote(ss.at[it], ssr.at[it], fs.at[it, 1], fr.at[it, 1], other_feat)
        sc.start()
        sc.wait_recv()
        sums = total + ssr[it]
        rr = to_col(sums[0:1])
        drr = to_col(sums[1:2])
        drp = to_col(sums[2:3])
        beta = jnp.where(it == 0, 0.0, rr / rr_old)
        dpp = drr + 2.0 * beta * drp + beta * beta * dpp_old
        p = r + beta * p
        p_ref[...] = p
        yc.wait_recv()
        yy = y[...] + yr[it].astype(F32) + beta * yold[...]
        yold[...] = yy
        wy = w_ref[...] * yy
        u = wy.astype(BF16)
        curve_own = to_row(jnp.sum(wy * yy, axis=1, keepdims=True))
        cs[it, 0] = jnp.broadcast_to(curve_own, (8, 128))

        reduce_start(cs, c_s, c_r)

        def term(slot):
            return jnp.dot(u, a[slot], preferred_element_type=F32)

        def to_die(k, dx):
            i = 2 * k + dx
            ds[it, i] = term(4 * k + 2 * dx + 1)
            copy = remote(ds.at[it, i], dr.at[it, i], d_s.at[it, i], d_r.at[it, i], die)
            copy.start()
            sent.append(copy)

        def from_die(k, dx):
            i = 2 * k + dx
            remote(
                ds.at[it, i], dr.at[it, i], d_s.at[it, i], d_r.at[it, i], die
            ).wait_recv()
            return dr[it, i]

        zorder = away + [0]
        for k in zorder:
            to_die(k, 1)
        reduce_x(cs, c_s, c_r)
        for k in zorder:
            part = term(4 * k + 2)
            xs[it, k] = (part + from_die(k, 1)).astype(BF16)
            copy = remote(xs.at[it, k], xr.at[it, k], x_s.at[it, k], x_r.at[it, k], side)
            copy.start()
            sent.append(copy)
        for k in zorder:
            to_die(k, 0)
        reduce_z(cs, c_s, c_r)
        for k in zorder:
            tt[k] = term(4 * k)

        def chip_sum(k):
            part = tt[k] + from_die(k, 0)
            remote(
                xs.at[it, k], xr.at[it, k], x_s.at[it, k], x_r.at[it, k], side
            ).wait_recv()
            return part + xr[it, k].astype(F32)

        for k in away:
            zs[it, k] = chip_sum(k).astype(BF16)
            copy = remote(
                zs.at[it, k], zr.at[it, depth - k],
                z_s.at[it, k], z_r.at[it, depth - k], dev(k, 0, 0),
            )
            copy.start()
            sent.append(copy)
        image = chip_sum(0) + damp * p
        curve_row = reduce_end(cs, c_s, c_r)
        alpha = rr / (to_col(curve_row[0:1]) + dpp)
        x_ref[...] += alpha * p
        for k in far:
            remote(
                zs.at[it, k], zr.at[it, k], z_s.at[it, k], z_r.at[it, k], die
            ).wait_recv()
            image = image + zr[it, k].astype(F32)
        r_ref[...] = r - alpha * image

        yc.wait_send()
        sc.wait_send()
        for copy in sent:
            copy.wait_send()
        return rr, dpp

    ones = jnp.ones((cols, 1), F32)
    lax.fori_loop(0, ITERS, iteration, (ones, jnp.zeros((cols, 1), F32)))


def fused(depth, design, flags, scales, damping, probes):
    rows_dev = design.shape[0]
    n = depth * 4
    total_rows = rows_dev * n
    cols, _, width = probes.shape
    vm = pl.BlockSpec(memory_space=pltpu.VMEM)
    v = pltpu.VMEM
    dma = pltpu.SemaphoreType.DMA
    out = jax.ShapeDtypeStruct((cols, width), F32)
    i2 = ITERS
    x, r = pl.pallas_call(
        functools.partial(solve_kernel, depth, total_rows),
        out_shape=(out, out),
        in_specs=[pl.BlockSpec(memory_space=pl.ANY)] * 5,
        out_specs=(vm, vm),
        scratch_shapes=[
            v((1, rows_dev), jnp.int32),
            v((1, rows_dev), F32),
            v((1, width), F32),
            v((cols, 1, width), F32),
            v((1, rows_dev), F32),
            v((n, rows_dev, width), BF16),
            v((i2, n, cols, width), BF16),
            v((i2, depth + 4, 8, 128), F32),
            v((cols, rows_dev), F32),
            v((cols, rows_dev), BF16),
            v((i2, cols, rows_dev), BF16),
            v((cols, rows_dev), F32),
            v((i2, 8, 128), F32),
            v((i2, 8, 128), F32),
            v((i2, 2 * depth, cols, width), F32),
            v((i2, 2 * depth, cols, width), F32),
            v((i2, depth, cols, width), BF16),
            v((i2, depth, cols, width), BF16),
            v((i2, depth, cols, width), BF16),
            v((i2, depth, cols, width), BF16),
            v((depth, cols, width), F32),
            v((i2, depth + 4, 8, 128), F32),
            v((cols, width), F32),
            dma((4,)),
            dma((n,)),
            dma((i2, n)),
            dma((i2, n)),
            dma((i2, depth + 1)),
            dma((i2, depth + 1)),
            dma((i2, 2)),
            dma((i2, 2)),
            dma((i2, 2 * depth)),
            dma((i2, 2 * depth)),
            dma((i2, depth)),
            dma((i2, depth)),
            dma((i2, depth)),
            dma((i2, depth)),
            dma((i2, depth + 1)),
            dma((i2, depth + 1)),
        ],
        compiler_params=pltpu.CompilerParams(
            collective_id=0, has_side_effects=True, vmem_limit_bytes=48 * 1024 * 1024
        ),
    )(design, flags.reshape(1, rows_dev), scales.reshape(1, rows_dev), damping, probes)
    return x.reshape(probes.shape), r.reshape(probes.shape)


def solution(mesh):
    placed = (P("rows", "feat"), P("rows"), P("rows"), P("feat", "rows"), P(None, "feat", "rows"))
    rows, feats = mesh.shape["rows"], mesh.shape["feat"]

    def body(design, flags, scales, damping, probes):
        fits = (
            feats == 2 and rows % 4 == 0 and 8 <= rows <= 16
            and probes.shape[2] % 256 == 0 and design.shape[0] % 256 == 0
            and design.size <= 1 << 23 and probes.shape[0] % 16 == 0
            and probes.shape[0] <= 32
        )
        if fits:
            return fused(rows // 4, design, flags, scales, damping, probes)
        return shards(design, flags, scales, damping, probes)

    return jax.shard_map(
        body,
        mesh=mesh,
        in_specs=placed,
        out_specs=(P(None, "feat", "rows"), P(None, "feat", "rows")),
        check_vma=False,
    )
```
